32 devices in a mesh: runs: 2 (over x), brick: 16 (over z, y, core).
Axes of the slice: x: 2, y: 2, z: 4, core: 2. Of those that a mesh axis runs over, the one named last changes fastest.
Arguments:
- grid: float32 [3, 8388608], P(None, ('runs', 'brick')), parts along dimension 1, may hold values from 0.2 to 4
- distribution: float32 [64, 16384], P(None, ('runs', 'brick')), parts along dimension 1, may hold values from 0.02 to 1
- owner_ids: int32 [16384, 1], P(('runs', 'brick')), parts along dimension 0, may hold values from 0 to 15; in each aligned block of 512 rows (0 to 511, 512 to 1023, ...) at most 64 rows name the same one
- coords: int32 [3, 16384], P(None, ('runs', 'brick')), parts along dimension 1, may hold values from 0 to 62
- fracs: float32 [3, 16384], P(None, ('runs', 'brick')), parts along dimension 1, may hold values from 0 to 1
- counts: int32 [16384], P(('runs', 'brick')), parts along dimension 0, may hold values from 1 to 4
- kernel: float32 [64, 64], replicated, may hold values from 0.002 to 0.2
- redist: float32 [64, 64], replicated, may hold values from 0.001 to 0.05
- shatter: float32 [64, 64], replicated, may hold values from 0.001 to 0.05
Outputs:
- updated: float32 [64, 16384], P(None, ('runs', 'brick')), parts along dimension 1
The draws below stay inside these ranges and needn't reach their ends.
There are 2 independent parts, one for each index of `runs`. The reference program is written for one: setup_inputs(seed, part) draws one part's arguments, and reference() takes and returns one part's arrays. A program takes and returns all parts, laid end to end along the dimension named above; an argument that names none is the same for every part. Nothing has to cross between parts.
Inputs may be any that keep to these rules, and one draw needn't show every extreme that they name: `owner_ids`: in the rows of one device at most 64 tracers name one brick, a bound that some block reaches of them.
All inputs are finite; a program needn't handle non-finite values.
Results may differ from the reference program's by a relative error of at most 0.0001.
Values sent between devices are 32-bit elements; how exact they have to be, the bound alone decides.
A program may use at most 256 MiB of HBM per device.

```python
import math
import jax
import jax.numpy as jnp
import numpy as np
from jax import lax

BINS = 64
BS = 64
TR_DEV = 512
CAP = 64
CELLS = 262144
TRACERS = 8192
N_BRICK = 16


def touch_ends(entries, key, smallest, top_value):
    place = [jax.random.randint(jax.random.fold_in(key, axis), (), 0, length) for axis, length in enumerate(entries.shape)]
    main_axis = entries.shape.index(max(entries.shape))
    neighbour = place[:main_axis] + [(place[main_axis] + 1) % entries.shape[main_axis]] + place[main_axis + 1:]
    return entries.at[tuple(place)].set(smallest).at[tuple(neighbour)].set(top_value)


def levels(stream_key, extent, split, least, top_value):
    factor_of = 1.0
    for position, shards_of in split:
        draws = jax.random.uniform(jax.random.fold_in(jax.random.fold_in(stream_key, 6), position), (shards_of,), jnp.float32, least / len(split), top_value / len(split))
        factor_of = factor_of * jnp.repeat(jnp.exp(draws), extent[position] // shards_of).reshape((-1,) + (1,) * (len(extent) - 1 - position))
    return factor_of


def shared_out(key, own, number, rows, amount, top, most, skew):
    order = jax.random.permutation(key, amount)
    heavy_load, usual = shares(amount, rows * top, most, skew, True), shares(amount, rows * top, most, skew, False)
    places = jnp.arange(amount)

    def named(lengths, rotation):
        used = int((lengths > 0).sum())
        fixed = max(1, used // 4)
        passed = fixed + (places - fixed + rotation * (used - fixed)) % max(1, amount - fixed)
        return jnp.zeros((amount,), jnp.int32).at[order[jnp.where(places < fixed, places, passed)]].set(jnp.asarray(lengths, jnp.int32))

    lengths = jnp.where(number % 4 == 0, named(heavy_load, number // 4), named(usual, number - number // 4 - 1))
    mixed = jax.random.permutation(jax.random.fold_in(own, 3), amount)
    giver, sink = mixed[0:amount // 2 * 2:2], mixed[1:amount // 2 * 2:2]
    margin = jnp.minimum(lengths[giver] - 1, most - lengths[sink]) // 2
    margin = jnp.where((giver == order[0]) | (sink == order[0]) | (lengths[sink] == 0), 0, jnp.maximum(margin, 0))
    passed = jax.random.randint(jax.random.fold_in(own, 4), (amount // 2,), 0, 1 << 20) % (margin + 1)
    lengths = lengths.at[giver].add(-passed).at[sink].add(passed)
    items = jnp.searchsorted(jnp.cumsum(lengths), jnp.arange(rows * top), side="right").astype(jnp.int32)
    table = items.reshape(top, rows).T
    table = table[jax.random.permutation(jax.random.fold_in(own, 1), rows)]
    rotation = jax.random.randint(jax.random.fold_in(own, 2), (rows, 1), 0, top)
    return jnp.take_along_axis(table, (jnp.arange(top)[None, :] + rotation) % top, axis=1)


def shares(count, total, reach, skew, full):
    portions = [(1 << 20) // math.isqrt(rank ** skew) + 1 for rank in range(1, count + 1)]
    largest = reach if full else min(reach, max(-(-total // count), total * portions[0] // sum(portions)))
    least = 1 if total - largest >= count - 1 else 0
    holding, surplus = [largest] + [least] * (count - 1), total - largest - least * (count - 1)
    while surplus > 0:
        candidates = [i for i in range(1, count) if holding[i] < largest] or [i for i in range(1, count) if holding[i] < reach]
        mass, left = sum([portions[i] for i in candidates]), surplus
        for i in candidates:
            more = min(reach - holding[i], max(1, left * portions[i] // mass), surplus)
            holding[i] = holding[i] + more
            surplus = surplus - more
    return np.array(holding)


def setup_inputs(seed: int = 0, part: int = 0) -> dict:
    seeds = jax.random.split(jax.random.key(seed), 10)
    part_keys = jax.random.split(jax.random.fold_in(seeds[9], part), 10)
    grid = jnp.clip(jnp.exp(math.log(4.0) - 2.9957323 * jax.random.uniform(part_keys[0], (3, CELLS * N_BRICK), jnp.float32) ** levels(part_keys[0], (3, CELLS * N_BRICK), ((1, 16),), -0.2, 0.2)), 0.2, 4.0)
    distribution = jnp.clip(jnp.exp(math.log(1.0) - 3.912023 * jax.random.uniform(part_keys[1], (BINS, TRACERS), jnp.float32) ** levels(part_keys[1], (BINS, TRACERS), ((1, 16),), -0.2, 0.2)), 0.02, 1.0)
    owner_ids_keys = jax.random.split(jax.random.fold_in(part_keys[2], 1), TRACERS // TR_DEV)
    owner_ids_turns = jax.random.permutation(jax.random.fold_in(part_keys[2], 3), TRACERS // TR_DEV)
    owner_ids = jax.vmap(lambda own, number: shared_out(jax.random.fold_in(part_keys[2], 2), own, number, TR_DEV, N_BRICK, 1, CAP, 2))(owner_ids_keys, owner_ids_turns).reshape((TRACERS, 1))
    coords = touch_ends(jax.random.randint(part_keys[3], (3, TRACERS), 0, BS - 1), jax.random.fold_in(part_keys[3], 1), 0, (BS - 1) - 1).astype(jnp.int32)
    fracs = jnp.clip(1.0 * jax.random.uniform(part_keys[4], (3, TRACERS), jnp.float32) ** levels(part_keys[4], (3, TRACERS), ((1, 16),), -0.2, 0.2), 0.0, 1.0)
    counts = touch_ends(jax.random.randint(part_keys[5], (TRACERS,), 1, 5), jax.random.fold_in(part_keys[5], 1), 1, 4).astype(jnp.int32)
    kernel = jnp.clip(jnp.exp(jax.random.uniform(seeds[6], (BINS, BINS), jnp.float32, math.log(0.002), math.log(0.2))), 0.002, 0.2)
    redist = jnp.clip(jnp.exp(jax.random.uniform(seeds[7], (BINS, BINS), jnp.float32, math.log(0.001), math.log(0.05))), 0.001, 0.05)
    shatter = jnp.clip(jnp.exp(jax.random.uniform(seeds[8], (BINS, BINS), jnp.float32, math.log(0.001), math.log(0.05))), 0.001, 0.05)
    return dict(grid=grid, distribution=distribution, owner_ids=owner_ids, coords=coords, fracs=fracs, counts=counts, kernel=kernel, redist=redist, shatter=shatter)


def corner_sum(fields, coords, fracs, side, offset):
    total = jnp.zeros(fracs.shape, jnp.float32)
    for corner in range(8):
        first = corner // 4
        second = corner // 2 % 2
        third = corner % 2
        weight = jnp.ones(fracs.shape[1:], jnp.float32)
        weight = weight * (fracs[0] if first else 1.0 - fracs[0])
        weight = weight * (fracs[1] if second else 1.0 - fracs[1])
        weight = weight * (fracs[2] if third else 1.0 - fracs[2])
        where = ((coords[0] + first) * side + coords[1] + second) * side + coords[2] + third + offset
        picked = jnp.take(fields, where.astype(jnp.int32), axis=1)
        total = total + weight[None] * picked
    return total

def advance(dist, coag, shat, steps, kernel, redist, shatter):
    step_size = 1.0 / jnp.maximum(steps, 1).astype(jnp.float32)
    for section in range(4):
        kernel_dot = jnp.einsum('ij,j...->i...', kernel, dist, precision=lax.Precision.HIGHEST)
        collided = dist * kernel_dot
        gain = coag * jnp.einsum('ij,j...->i...', redist, collided, precision=lax.Precision.HIGHEST)
        gain = gain + shat * jnp.einsum('ij,j...->i...', shatter, dist, precision=lax.Precision.HIGHEST)
        loss = coag * kernel_dot + shat
        fresh = (dist + step_size * gain) / (1.0 + step_size * loss)
        dist = jnp.where(steps >= section + 1, fresh, dist)
    return dist

def reference(grid, distribution, owner_ids, coords, fracs, counts, kernel, redist, shatter):
    owner = owner_ids[:, 0]
    sampled = corner_sum(grid, coords, fracs, BS, owner * (BS * BS * BS))
    coag = sampled[0] * jnp.sqrt(sampled[1])
    shat = sampled[2] * sampled[1]
    return advance(distribution, coag, shat, counts, kernel, redist, shatter)
```

```python
import functools

import jax
import jax.numpy as jnp
from jax import lax
from jax.experimental import pallas as pl
from jax.experimental.pallas import tpu as pltpu
from jax.sharding import PartitionSpec as P

BS = 64
LANES = 128
HALF = LANES // 2
STEPS = 4
MESH = pl.DeviceIdType.MESH


def iota(shape, dim):
    return lax.broadcasted_iota(jnp.int32, shape, dim)


def pieces(x, count=3):
    out = []
    for _ in range(count):
        high = x.astype(jnp.bfloat16)
        out.append(high)
        x = x - high.astype(jnp.float32)
    return out


def mxu(a, b, contract=((1,), (0,))):
    return lax.dot_general(a, b, (contract, ((), ())), preferred_element_type=jnp.float32)


NT = ((1,), (1,))


def partner(me, d, n):
    return {"brick": lax.rem(me + d, n)}


def greet(me, n):
    barrier = pltpu.get_barrier_semaphore()
    for d in range(1, n):
        pl.semaphore_signal(barrier, inc=1, device_id=partner(me, d, n), device_id_type=MESH)
    return barrier


def request(
    n, owner_ref, coords_ref, fracs_ref, got_ref, index_ref, rank_ref,
    pad, send, recv, send_sem, recv_sem,
):
    me = lax.axis_index("brick")
    barrier = greet(me, n)

    tracers = owner_ref.shape[1]
    rel = owner_ref[...] - me
    rel = jnp.where(rel < 0, rel + n, rel)
    onehot = jnp.where(iota((n, tracers), 0) == rel, 1.0, 0.0)
    upto = jnp.where(iota((LANES, LANES), 0) <= iota((LANES, LANES), 1), 1.0, 0.0)
    upto = upto.astype(jnp.bfloat16)
    running = jnp.zeros((n, 1), jnp.float32)
    ranks = []
    for start in range(0, tracers, LANES):
        part = onehot[:, start : start + LANES]
        counted = mxu(part.astype(jnp.bfloat16), upto) + running
        running = counted[:, LANES - 1 :]
        ranks.append(jnp.sum(part * counted, axis=0, keepdims=True))
    rank = jnp.concatenate(ranks, axis=1).astype(jnp.int32) - 1
    rank_ref[...] = rank
    placed = (iota((LANES, tracers), 0) % HALF) == rank
    placed = jnp.where(placed, 1.0, 0.0).astype(jnp.bfloat16)

    pad[...] = jnp.zeros_like(pad)
    for row in (0, 4):
        pad[0, row : row + 3, :] = coords_ref[...].astype(jnp.float32)
        pad[1, row : row + 3, :] = fracs_ref[...]
    dest = (iota((4 * n, tracers), 0) // 4) == rel
    rows = [pad[0].astype(jnp.bfloat16)] + pieces(pad[1])
    left = []
    for x in rows:
        x = jnp.concatenate([x.astype(jnp.float32)] * (n // 2), axis=0)
        left.append(jnp.where(dest, x, 0.0).astype(jnp.bfloat16))
    packed = mxu(jnp.concatenate(left, axis=0), placed, NT)
    four = 4 * n
    packed = jnp.where(
        iota((four, LANES), 1) < HALF,
        packed[:four],
        packed[four : 2 * four] + packed[2 * four : 3 * four] + packed[3 * four :],
    )
    for d in range(n):
        send[d] = packed[4 * d : 4 * d + 4]
    recv[0] = packed[:4]

    pl.semaphore_wait(barrier, n - 1)
    copies = []
    for d in range(1, n):
        copy = pltpu.make_async_remote_copy(
            src_ref=send.at[d],
            dst_ref=recv.at[d],
            send_sem=send_sem.at[d],
            recv_sem=recv_sem.at[d],
            device_id=partner(me, d, n),
            device_id_type=MESH,
        )
        copy.start()
        copies.append(copy)
    for copy in copies:
        copy.wait()

    low = iota((n, LANES), 1) < HALF
    ci = jnp.where(low, recv[:, 0, :], 0.0).astype(jnp.int32)
    cj = jnp.where(low, recv[:, 1, :], 0.0).astype(jnp.int32)
    base = ci * (BS * BS // LANES)
    index_ref[:n] = base + (cj >> 1)
    index_ref[n:] = base + ((cj + 1) >> 1)
    got_ref[...] = recv[...]


def answer(
    n, cap, index_ref, got_ref, rank_ref, owner_ref, counts_ref, dist_ref, kernel_ref,
    redist_ref, shatter_ref, cells, out_ref,
    w0_ref, w1_ref, stage, rsend, rrecv, rsend_sem, rrecv_sem,
):
    me = lax.axis_index("brick")
    barrier = greet(me, n)

    stage[...] = jnp.zeros_like(stage)
    first, second, third = got_ref[:, 0, :], got_ref[:, 1, :], got_ref[:, 2, :]
    in_low = iota((n, LANES), 1) < HALF
    cj = jnp.where(in_low, second, 0.0).astype(jnp.int32)
    f0 = pltpu.roll(first, HALF, 1)
    f1 = pltpu.roll(second, HALF, 1)
    f2 = pltpu.roll(third, HALF, 1)
    even = jnp.where((cj & 1) == 0, 1.0 - f1, f1)
    columns = jnp.concatenate([third, f2, even, f0], axis=0).T
    lanes = iota((cap, LANES), 1)
    inner = (lanes % HALF).astype(jnp.float32)
    lower = lanes < HALF
    for s in range(n):
        ck = columns[:cap, s : s + 1]
        a2 = columns[:cap, n + s : n + s + 1]
        ae = columns[:cap, 2 * n + s : 2 * n + s + 1]
        a0 = columns[:cap, 3 * n + s : 3 * n + s + 1]
        w = jnp.where(inner == ck, 1.0 - a2, jnp.where(inner == ck + 1.0, a2, 0.0))
        w = w * jnp.where(lower, ae, 1.0 - ae)
        w0_ref[s * cap : (s + 1) * cap, :] = w * (1.0 - a0)
        w1_ref[s * cap : (s + 1) * cap, :] = w * a0

    plane = BS * BS // LANES
    front = iota((3, LANES), 1) < HALF

    def one(s, carry):
        for c in range(cap):
            up = index_ref[s, c]
            dn = index_ref[n + s, c]
            near = jnp.where(front, cells[dn], cells[up])
            far = jnp.where(front, cells[dn + plane], cells[up + plane])
            at = s * cap + c
            acc = near * w0_ref[pl.ds(at, 1), :] + far * w1_ref[pl.ds(at, 1), :]
            stage[pl.ds(s * 4 * HALF + c, 3, stride=HALF), :] = acc
        return carry

    lax.fori_loop(0, n, one, 0)

    ones = jnp.ones((8, LANES), jnp.bfloat16)
    for s in range(n):
        block = stage[s * 4 * HALF : (s + 1) * 4 * HALF, :]
        total = sum(mxu(ones, p, NT) for p in pieces(block))
        rsend[s, 0:1] = total[:1, :LANES]
        rsend[s, 1:2] = total[:1, LANES:]
    rrecv[0] = rsend[0]
    pl.semaphore_wait(barrier, n - 1)
    copies = []
    for d in range(1, n):
        copy = pltpu.make_async_remote_copy(
            src_ref=rsend.at[d],
            dst_ref=rrecv.at[d],
            send_sem=rsend_sem.at[d],
            recv_sem=rrecv_sem.at[d],
            device_id=partner(me, n - d, n),
            device_id_type=MESH,
        )
        copy.start()
        copies.append(copy)

    tracers = owner_ref.shape[1]
    rel = owner_ref[...] - me
    rel = jnp.where(rel < 0, rel + n, rel)
    onehot = jnp.where(iota((n, tracers), 0) == rel, 1.0, 0.0)
    placed = (iota((LANES, tracers), 0) % HALF) == rank_ref[...]
    placed = jnp.where(placed, 1.0, 0.0).astype(jnp.bfloat16)
    for copy in copies:
        copy.wait()

    pair, single = rrecv[:, 0, :], rrecv[:, 1, :]
    spread = jnp.concatenate(
        [
            jnp.where(in_low, pair, 0.0),
            jnp.where(in_low, 0.0, pair),
            jnp.where(in_low, single, 0.0),
        ],
        axis=0,
    )
    found = sum(mxu(p, placed) for p in pieces(spread))
    sampled = [
        jnp.sum(found[f * n : (f + 1) * n] * onehot, axis=0, keepdims=True) for f in range(3)
    ]
    coag = sampled[0] * jnp.sqrt(sampled[1])
    shat = sampled[2] * sampled[1]
    steps = counts_ref[...]
    h = 1.0 / jnp.maximum(steps, 1).astype(jnp.float32)
    dist = dist_ref[...]

    def full(a, b):
        return jnp.dot(a, b, precision=lax.Precision.HIGHEST, preferred_element_type=jnp.float32)

    for section in range(STEPS):
        dot = full(kernel_ref[...], dist)
        gain = coag * full(redist_ref[...], dist * dot)
        gain = gain + shat * full(shatter_ref[...], dist)
        loss = coag * dot + shat
        fresh = (dist + h * gain) / (1.0 + h * loss)
        dist = jnp.where(steps >= section + 1, fresh, dist)
    out_ref[...] = dist


def shards(grid, distribution, owner_ids, coords, fracs, counts, kernel, redist, shatter):
    n = lax.axis_size("brick")
    bins, tracers = distribution.shape
    cap = 2 * tracers // n
    assert cap <= HALF and n % 2 == 0 and tracers % LANES == 0
    vmem = pl.BlockSpec(memory_space=pltpu.VMEM)
    smem = pl.BlockSpec(memory_space=pltpu.SMEM)
    f32 = jnp.float32
    owner = owner_ids.reshape(1, tracers)
    got, index, rank = pl.pallas_call(
        functools.partial(request, n),
        out_shape=(
            jax.ShapeDtypeStruct((n, 4, LANES), f32),
            jax.ShapeDtypeStruct((2 * n, LANES), jnp.int32),
            jax.ShapeDtypeStruct((1, tracers), jnp.int32),
        ),
        in_specs=[vmem] * 3,
        out_specs=(vmem, vmem, vmem),
        scratch_shapes=[
            pltpu.VMEM((2, 8, tracers), f32),
            pltpu.VMEM((n, 4, LANES), f32),
            pltpu.VMEM((n, 4, LANES), f32),
            pltpu.SemaphoreType.DMA((n,)),
            pltpu.SemaphoreType.DMA((n,)),
        ],
        compiler_params=pltpu.CompilerParams(
            collective_id=0, has_side_effects=True, vmem_limit_bytes=8 * 1024 * 1024
        ),
        name="request",
    )(owner, coords, fracs)
    cells = jnp.swapaxes(grid.reshape(grid.shape[0], -1, LANES), 0, 1)
    return pl.pallas_call(
        functools.partial(answer, n, cap),
        out_shape=jax.ShapeDtypeStruct((bins, tracers), f32),
        in_specs=[smem] + [vmem] * 9,
        out_specs=vmem,
        scratch_shapes=[
            pltpu.VMEM((n * cap, LANES), f32),
            pltpu.VMEM((n * cap, LANES), f32),
            pltpu.VMEM((n * 4 * HALF, LANES), f32),
            pltpu.VMEM((n, 2, LANES), f32),
            pltpu.VMEM((n, 2, LANES), f32),
            pltpu.SemaphoreType.DMA((n,)),
            pltpu.SemaphoreType.DMA((n,)),
        ],
        compiler_params=pltpu.CompilerParams(
            collective_id=1, has_side_effects=True, vmem_limit_bytes=24 * 1024 * 1024
        ),
        name="answer",
    )(
        index, got, rank, owner, counts.reshape(1, tracers), distribution, kernel, redist,
        shatter, cells,
    )


def solution(mesh):
    in_specs = (
        P(None, ("runs", "brick")),
        P(None, ("runs", "brick")),
        P(("runs", "brick"), None),
        P(None, ("runs", "brick")),
        P(None, ("runs", "brick")),
        P(("runs", "brick")),
        P(),
        P(),
        P(),
    )
    out_specs = P(None, ("runs", "brick"))
    return jax.shard_map(shards, mesh=mesh, in_specs=in_specs, out_specs=out_specs, check_vma=False)
```

```python
import functools

import jax
import jax.numpy as jnp
from jax import lax
from jax.experimental import pallas as pl
from jax.experimental.pallas import tpu as pltpu
from jax.sharding import PartitionSpec as P

BS = 64
LANES = 128
HALF = LANES // 2
STEPS = 4
KEPT = 6
GROUPS = 4
MESH = pl.DeviceIdType.MESH


def iota(shape, dim):
    return lax.broadcasted_iota(jnp.int32, shape, dim)


def pieces(x, count=3):
    out = []
    for _ in range(count):
        high = x.astype(jnp.bfloat16)
        out.append(high)
        x = x - high.astype(jnp.float32)
    return out


def mxu(a, b, contract=((1,), (0,))):
    return lax.dot_general(a, b, (contract, ((), ())), preferred_element_type=jnp.float32)


NT = ((1,), (1,))


def wide(x):
    high, low = pieces(x, 2)
    return jnp.concatenate([high, high, low], axis=1)


def tall(x):
    high, low = pieces(x, 2)
    return jnp.concatenate([high, low, high], axis=0)


def partner(me, d, n):
    return {"brick": lax.rem(me + d, n)}


def greet(me, n):
    barrier = pltpu.get_barrier_semaphore()
    for d in range(1, n):
        pl.semaphore_signal(barrier, inc=1, device_id=partner(me, d, n), device_id_type=MESH)
    return barrier


def request(
    n, owner_hbm, coords_hbm, fracs_hbm, *refs,
):
    kept_hbm, (got_ref, index_ref, rank_ref, owner_ref) = refs[:KEPT], refs[KEPT : KEPT + 4]
    kept_refs = refs[KEPT + 4 : 2 * KEPT + 4]
    coords_ref, fracs_ref, pad, send, recv, load_sem, send_sem, recv_sem = refs[2 * KEPT + 4 :]
    me = lax.axis_index("brick")
    sources = (owner_hbm, coords_hbm, fracs_hbm) + kept_hbm
    targets = (owner_ref, coords_ref, fracs_ref) + kept_refs
    loads = [
        pltpu.make_async_copy(a, b, load_sem.at[i]) for i, (a, b) in enumerate(zip(sources, targets))
    ]
    for load in loads:
        load.start()
    barrier = greet(me, n)
    for load in loads[:3]:
        load.wait()

    tracers = owner_ref.shape[1]
    rel = owner_ref[...] - me
    rel = jnp.where(rel < 0, rel + n, rel)
    onehot = jnp.where(iota((n, tracers), 0) == rel, 1.0, 0.0)
    upto = jnp.where(iota((LANES, LANES), 0) <= iota((LANES, LANES), 1), 1.0, 0.0)
    upto = upto.astype(jnp.bfloat16)
    running = jnp.zeros((n, 1), jnp.float32)
    ranks = []
    for start in range(0, tracers, LANES):
        part = onehot[:, start : start + LANES]
        counted = mxu(part.astype(jnp.bfloat16), upto) + running
        running = counted[:, LANES - 1 :]
        ranks.append(jnp.sum(part * counted, axis=0, keepdims=True))
    rank = jnp.concatenate(ranks, axis=1).astype(jnp.int32) - 1
    rank_ref[...] = rank
    placed = (iota((LANES, tracers), 0) % HALF) == rank
    placed = jnp.where(placed, 1.0, 0.0).astype(jnp.bfloat16)

    pad[...] = jnp.zeros_like(pad)
    for row in (0, 4):
        pad[0, row : row + 3, :] = coords_ref[...].astype(jnp.float32)
        pad[1, row : row + 3, :] = fracs_ref[...]
    dest = (iota((4 * n, tracers), 0) // 4) == rel
    rows = [pad[0].astype(jnp.bfloat16)] + pieces(pad[1])
    left = []
    for x in rows:
        x = jnp.concatenate([x.astype(jnp.float32)] * (n // 2), axis=0)
        left.append(jnp.where(dest, x, 0.0).astype(jnp.bfloat16))
    packed = mxu(jnp.concatenate(left, axis=0), placed, NT)
    four = 4 * n
    packed = jnp.where(
        iota((four, LANES), 1) < HALF,
        packed[:four],
        packed[four : 2 * four] + packed[2 * four : 3 * four] + packed[3 * four :],
    )
    for d in range(n):
        send[d] = packed[4 * d : 4 * d + 4]
    recv[0] = packed[:4]

    pl.semaphore_wait(barrier, n - 1)
    copies = []
    for d in range(1, n):
        copy = pltpu.make_async_remote_copy(
            src_ref=send.at[d],
            dst_ref=recv.at[d],
            send_sem=send_sem.at[d],
            recv_sem=recv_sem.at[d],
            device_id=partner(me, d, n),
            device_id_type=MESH,
        )
        copy.start()
        copies.append(copy)
    for copy in copies:
        copy.wait()

    low = iota((n, LANES), 1) < HALF
    ci = jnp.where(low, recv[:, 0, :], 0.0).astype(jnp.int32)
    cj = jnp.where(low, recv[:, 1, :], 0.0).astype(jnp.int32)
    base = ci * (BS * BS // LANES)
    index_ref[:n] = base + (cj >> 1)
    index_ref[n:] = base + ((cj + 1) >> 1)
    got_ref[...] = recv[...]
    for load in loads[3:]:
        load.wait()


def answer(
    n, cap, index_ref, got_ref, rank_ref, owner_ref, cells, counts_ref, dist_ref, kernel_ref,
    redist_ref, shatter_ref, out_ref,
    w0_ref, w1_ref, stage, rsend, rrecv, rsend_sem, rrecv_sem,
):
    me = lax.axis_index("brick")
    barrier = greet(me, n)

    first, second, third = got_ref[:, 0, :], got_ref[:, 1, :], got_ref[:, 2, :]
    in_low = iota((n, LANES), 1) < HALF
    cj = jnp.where(in_low, second, 0.0).astype(jnp.int32)
    f0 = pltpu.roll(first, HALF, 1)
    f1 = pltpu.roll(second, HALF, 1)
    f2 = pltpu.roll(third, HALF, 1)
    even = jnp.where((cj & 1) == 0, 1.0 - f1, f1)
    columns = jnp.concatenate([third, f2, even, f0], axis=0).T
    lanes = iota((cap, LANES), 1)
    inner = (lanes % HALF).astype(jnp.float32)
    lower = lanes < HALF
    for s in range(n):
        ck = columns[:cap, s : s + 1]
        a2 = columns[:cap, n + s : n + s + 1]
        ae = columns[:cap, 2 * n + s : 2 * n + s + 1]
        a0 = columns[:cap, 3 * n + s : 3 * n + s + 1]
        w = jnp.where(inner == ck, 1.0 - a2, jnp.where(inner == ck + 1.0, a2, 0.0))
        w = w * jnp.where(lower, ae, 1.0 - ae)
        w0_ref[s * cap : (s + 1) * cap, :] = w * (1.0 - a0)
        w1_ref[s * cap : (s + 1) * cap, :] = w * a0

    plane = BS * BS // LANES
    front = iota((3, LANES), 1) < HALF

    def one(s, carry):
        for c in range(cap):
            up = index_ref[s, c]
            dn = index_ref[n + s, c]
            near = jnp.where(front, cells[dn], cells[up])
            far = jnp.where(front, cells[dn + plane], cells[up + plane])
            at = s * cap + c
            acc = near * w0_ref[pl.ds(at, 1), :] + far * w1_ref[pl.ds(at, 1), :]
            stage[pl.ds(s * 3 * HALF + c, 3, stride=HALF), :] = acc
        return carry

    ones = jnp.ones((8, LANES), jnp.bfloat16)
    blank = jnp.zeros((1, HALF), jnp.float32)
    size = n // GROUPS
    copies = []
    for g in range(GROUPS):
        lax.fori_loop(g * size, (g + 1) * size, one, 0)
        for s in range(g * size, (g + 1) * size):
            block = stage[s * 3 * HALF : (s + 1) * 3 * HALF, :]
            total = sum(mxu(ones, p, NT) for p in pieces(block))[:1]
            rsend[s, 0:1] = total[:, :LANES]
            rsend[s, 1:2] = jnp.concatenate([total[:, LANES:], blank], axis=1)
        if g == 0:
            pl.semaphore_wait(barrier, n - 1)
            rrecv[0] = rsend[0]
        for d in range(max(1, g * size), (g + 1) * size):
            copy = pltpu.make_async_remote_copy(
                src_ref=rsend.at[d],
                dst_ref=rrecv.at[d],
                send_sem=rsend_sem.at[d],
                recv_sem=rrecv_sem.at[d],
                device_id=partner(me, n - d, n),
                device_id_type=MESH,
            )
            copy.start()
            copies.append(copy)

    tracers = owner_ref.shape[1]
    rel = owner_ref[...] - me
    rel = jnp.where(rel < 0, rel + n, rel)
    onehot = jnp.where(iota((n, tracers), 0) == rel, 1.0, 0.0)
    placed = (iota((LANES, tracers), 0) % HALF) == rank_ref[...]
    placed = jnp.where(placed, 1.0, 0.0).astype(jnp.bfloat16)
    steps = counts_ref[...]
    h = 1.0 / jnp.maximum(steps, 1).astype(jnp.float32)
    dist = dist_ref[...]
    bins = dist.shape[0]
    both = wide(jnp.concatenate([kernel_ref[...], shatter_ref[...]], axis=0))
    moved = wide(redist_ref[...])

    def products(dist):
        out = mxu(both, tall(dist))
        dot, broken = out[:bins], out[bins:]
        return dot, broken, mxu(moved, tall(dist * dot))

    ready = products(dist)
    for copy in copies:
        copy.wait()

    pair, single = rrecv[:, 0, :], rrecv[:, 1, :]
    spread = jnp.concatenate(
        [
            jnp.where(in_low, pair, 0.0),
            jnp.where(in_low, 0.0, pair),
            jnp.where(in_low, single, 0.0),
        ],
        axis=0,
    )
    found = sum(mxu(p, placed) for p in pieces(spread))
    sampled = [
        jnp.sum(found[f * n : (f + 1) * n] * onehot, axis=0, keepdims=True) for f in range(3)
    ]
    coag = sampled[0] * jnp.sqrt(sampled[1])
    shat = sampled[2] * sampled[1]
    for section in range(STEPS):
        dot, broken, back = ready if section == 0 else products(dist)
        gain = coag * back + shat * broken
        loss = coag * dot + shat
        fresh = (dist + h * gain) / (1.0 + h * loss)
        dist = jnp.where(steps >= section + 1, fresh, dist)
    out_ref[...] = dist


def shards(grid, distribution, owner_ids, coords, fracs, counts, kernel, redist, shatter):
    n = lax.axis_size("brick")
    bins, tracers = distribution.shape
    cap = 2 * tracers // n
    assert cap <= HALF and n % 2 == 0 and tracers % LANES == 0
    vmem = pl.BlockSpec(memory_space=pltpu.VMEM)
    smem = pl.BlockSpec(memory_space=pltpu.SMEM)
    f32 = jnp.float32
    hbm = pl.BlockSpec(memory_space=pltpu.HBM)
    kept = (
        jnp.swapaxes(grid.reshape(grid.shape[0], -1, LANES), 0, 1),
        counts.reshape(1, tracers), distribution, kernel, redist, shatter,
    )
    assert len(kept) == KEPT
    got, index, rank, owner, *kept = pl.pallas_call(
        functools.partial(request, n),
        out_shape=(
            jax.ShapeDtypeStruct((n, 4, LANES), f32),
            jax.ShapeDtypeStruct((2 * n, LANES), jnp.int32),
            jax.ShapeDtypeStruct((1, tracers), jnp.int32),
            jax.ShapeDtypeStruct((1, tracers), jnp.int32),
            *[jax.ShapeDtypeStruct(x.shape, x.dtype) for x in kept],
        ),
        in_specs=[hbm] * (3 + KEPT),
        out_specs=(vmem,) * (4 + KEPT),
        scratch_shapes=[
            pltpu.VMEM(coords.shape, jnp.int32),
            pltpu.VMEM(fracs.shape, f32),
            pltpu.VMEM((2, 8, tracers), f32),
            pltpu.VMEM((n, 4, LANES), f32),
            pltpu.VMEM((n, 4, LANES), f32),
            pltpu.SemaphoreType.DMA((3 + KEPT,)),
            pltpu.SemaphoreType.DMA((n,)),
            pltpu.SemaphoreType.DMA((n,)),
        ],
        compiler_params=pltpu.CompilerParams(
            collective_id=0, has_side_effects=True, vmem_limit_bytes=16 * 1024 * 1024
        ),
        name="request",
    )(*[pltpu.with_memory_space_constraint(x, pltpu.HBM) for x in (owner_ids.reshape(1, tracers), coords, fracs, *kept)])
    return pl.pallas_call(
        functools.partial(answer, n, cap),
        out_shape=jax.ShapeDtypeStruct((bins, tracers), f32),
        in_specs=[smem] + [vmem] * (3 + KEPT),
        out_specs=vmem,
        scratch_shapes=[
            pltpu.VMEM((n * cap, LANES), f32),
            pltpu.VMEM((n * cap, LANES), f32),
            pltpu.VMEM((n * 3 * HALF, LANES), f32),
            pltpu.VMEM((n, 2, LANES), f32),
            pltpu.VMEM((n, 2, LANES), f32),
            pltpu.SemaphoreType.DMA((n,)),
            pltpu.SemaphoreType.DMA((n,)),
        ],
        compiler_params=pltpu.CompilerParams(
            collective_id=1, has_side_effects=True, vmem_limit_bytes=24 * 1024 * 1024
        ),
        name="answer",
    )(index, got, rank, owner, *kept)


def solution(mesh):
    in_specs = (
        P(None, ("runs", "brick")),
        P(None, ("runs", "brick")),
        P(("runs", "brick"), None),
        P(None, ("runs", "brick")),
        P(None, ("runs", "brick")),
        P(("runs", "brick")),
        P(),
        P(),
        P(),
    )
    out_specs = P(None, ("runs", "brick"))
    return jax.shard_map(shards, mesh=mesh, in_specs=in_specs, out_specs=out_specs, check_vma=False)
```

```python
import functools

import jax
import jax.numpy as jnp
from jax import lax
from jax.experimental import pallas as pl
from jax.experimental.pallas import tpu as pltpu
from jax.sharding import PartitionSpec as P

BS = 64
LANES = 128
HALF = LANES // 2
STEPS = 4
KEPT = 6
MESH = pl.DeviceIdType.MESH


def iota(shape, dim):
    return lax.broadcasted_iota(jnp.int32, shape, dim)


def pieces(x, count=3):
    out = []
    for _ in range(count):
        high = x.astype(jnp.bfloat16)
        out.append(high)
        x = x - high.astype(jnp.float32)
    return out


def mxu(a, b, contract=((1,), (0,))):
    return lax.dot_general(a, b, (contract, ((), ())), preferred_element_type=jnp.float32)


NT = ((1,), (1,))


def wide(x):
    high, low = pieces(x, 2)
    return jnp.concatenate([high, high, low], axis=1)


def tall(x):
    high, low = pieces(x, 2)
    return jnp.concatenate([high, low, high], axis=0)


def partner(me, d, n):
    return {"brick": lax.rem(me + d, n)}


def greet(me, n):
    barrier = pltpu.get_barrier_semaphore()
    for d in range(1, n):
        pl.semaphore_signal(barrier, inc=1, device_id=partner(me, d, n), device_id_type=MESH)
    return barrier


def request(
    n, owner_hbm, coords_hbm, fracs_hbm, *refs,
):
    kept_hbm, (got_ref, index_ref, rank_ref, owner_ref) = refs[:KEPT], refs[KEPT : KEPT + 4]
    kept_refs = refs[KEPT + 4 : 2 * KEPT + 4]
    coords_ref, fracs_ref, pad, send, recv, load_sem, send_sem, recv_sem = refs[2 * KEPT + 4 :]
    me = lax.axis_index("brick")
    sources = (owner_hbm, coords_hbm, fracs_hbm) + kept_hbm
    targets = (owner_ref, coords_ref, fracs_ref) + kept_refs
    loads = [
        pltpu.make_async_copy(a, b, load_sem.at[i]) for i, (a, b) in enumerate(zip(sources, targets))
    ]
    for load in loads:
        load.start()
    barrier = greet(me, n)
    for load in loads[:3]:
        load.wait()

    tracers = owner_ref.shape[1]
    rel = owner_ref[...] - me
    rel = jnp.where(rel < 0, rel + n, rel)
    onehot = jnp.where(iota((n, tracers), 0) == rel, 1.0, 0.0)
    upto = jnp.where(iota((LANES, LANES), 0) <= iota((LANES, LANES), 1), 1.0, 0.0)
    upto = upto.astype(jnp.bfloat16)
    running = jnp.zeros((n, 1), jnp.float32)
    ranks = []
    for start in range(0, tracers, LANES):
        part = onehot[:, start : start + LANES]
        counted = mxu(part.astype(jnp.bfloat16), upto) + running
        running = counted[:, LANES - 1 :]
        ranks.append(jnp.sum(part * counted, axis=0, keepdims=True))
    rank = jnp.concatenate(ranks, axis=1).astype(jnp.int32) - 1
    rank_ref[...] = rank
    placed = (iota((LANES, tracers), 0) % HALF) == rank
    placed = jnp.where(placed, 1.0, 0.0).astype(jnp.bfloat16)

    pad[...] = jnp.zeros_like(pad)
    for row in (0, 4):
        pad[0, row : row + 3, :] = coords_ref[...].astype(jnp.float32)
        pad[1, row : row + 3, :] = fracs_ref[...]
    dest = (iota((4 * n, tracers), 0) // 4) == rel
    rows = [pad[0].astype(jnp.bfloat16)] + pieces(pad[1])
    left = []
    for x in rows:
        x = jnp.concatenate([x.astype(jnp.float32)] * (n // 2), axis=0)
        left.append(jnp.where(dest, x, 0.0).astype(jnp.bfloat16))
    packed = mxu(jnp.concatenate(left, axis=0), placed, NT)
    four = 4 * n
    packed = jnp.where(
        iota((four, LANES), 1) < HALF,
        packed[:four],
        packed[four : 2 * four] + packed[2 * four : 3 * four] + packed[3 * four :],
    )
    for d in range(n):
        send[d] = packed[4 * d : 4 * d + 4]
    recv[0] = packed[:4]

    pl.semaphore_wait(barrier, n - 1)
    copies = []
    for d in range(1, n):
        copy = pltpu.make_async_remote_copy(
            src_ref=send.at[d],
            dst_ref=recv.at[d],
            send_sem=send_sem.at[d],
            recv_sem=recv_sem.at[d],
            device_id=partner(me, d, n),
            device_id_type=MESH,
        )
        copy.start()
        copies.append(copy)
    for copy in copies:
        copy.wait()

    low = iota((n, LANES), 1) < HALF
    ci = jnp.where(low, recv[:, 0, :], 0.0).astype(jnp.int32)
    cj = jnp.where(low, recv[:, 1, :], 0.0).astype(jnp.int32)
    base = ci * (BS * BS // LANES)
    index_ref[:n] = base + (cj >> 1)
    index_ref[n:] = base + ((cj + 1) >> 1)
    got_ref[...] = recv[...]
    for load in loads[3:]:
        load.wait()


def answer(
    n, cap, index_ref, got_ref, rank_ref, owner_ref, cells, counts_ref, dist_ref, kernel_ref,
    redist_ref, shatter_ref, out_ref,
    index_s, wa0, wa1, wb0, wb1, stage_a, stage_b, rsend, rrecv, index_sem, rsend_sem, rrecv_sem,
):
    me = lax.axis_index("brick")
    index_copy = pltpu.make_async_copy(index_ref, index_s, index_sem)
    index_copy.start()
    barrier = greet(me, n)
    in_low = iota((n, LANES), 1) < HALF
    lanes = iota((cap, LANES), 1)
    inner = (lanes % HALF).astype(jnp.float32)
    lower = lanes < HALF
    plane = BS * BS // LANES
    front = iota((3, LANES), 1) < HALF
    ones = jnp.ones((8, 2 * LANES), jnp.bfloat16)
    blank = jnp.zeros((1, HALF), jnp.float32)

    def weigh(d, w0_ref, w1_ref):
        block = got_ref[d]
        turned = pltpu.roll(block, HALF, 1)
        odd = (block.astype(jnp.int32) & 1) == 1
        even = jnp.where(odd, turned, 1.0 - turned)
        columns = jnp.concatenate([block, even], axis=0).T
        ck = columns[:cap, 2:3]
        ae = columns[:cap, 5:6]
        a0 = columns[HALF : HALF + cap, 0:1]
        a2 = columns[HALF : HALF + cap, 2:3]
        w = jnp.where(inner == ck, 1.0 - a2, jnp.where(inner == ck + 1.0, a2, 0.0))
        w = w * jnp.where(lower, ae, 1.0 - ae)
        w0_ref[...] = w * (1.0 - a0)
        w1_ref[...] = w * a0

    def gather(d, w0_ref, w1_ref, stage):
        for c in range(cap):
            up = index_s[d, c]
            dn = index_s[n + d, c]
            near = jnp.where(front, cells[dn], cells[up])
            far = jnp.where(front, cells[dn + plane], cells[up + plane])
            acc = near * w0_ref[c : c + 1, :] + far * w1_ref[c : c + 1, :]
            stage[pl.ds(c, 3, stride=HALF), :] = acc

    def reduce(stage):
        total = mxu(ones, jnp.concatenate(pieces(stage[...], 2), axis=1), NT)[:1]
        return total[:, :LANES], jnp.concatenate([total[:, LANES:], blank], axis=1)

    def back(d):
        return pltpu.make_async_remote_copy(
            src_ref=rsend.at[d],
            dst_ref=rrecv.at[d],
            send_sem=rsend_sem.at[d],
            recv_sem=rrecv_sem.at[d],
            device_id=partner(me, n - d, n),
            device_id_type=MESH,
        )

    def finish(d, stage):
        rsend[d, 0:1], rsend[d, 1:2] = reduce(stage)
        back(d).start()

    if cap < HALF:
        stage_a[...] = jnp.zeros_like(stage_a)
        stage_b[...] = jnp.zeros_like(stage_b)
    weigh(1, wa0, wa1)
    index_copy.wait()
    gather(1, wa0, wa1, stage_a)
    weigh(2, wb0, wb1)
    pl.semaphore_wait(barrier, n - 1)

    def two(i, carry):
        d = 2 * i + 2
        weigh(d + 1, wa0, wa1)
        gather(d, wb0, wb1, stage_b)
        finish(d - 1, stage_a)
        weigh(lax.rem(d + 2, n), wb0, wb1)
        gather(d + 1, wa0, wa1, stage_a)
        finish(d, stage_b)
        return carry

    lax.fori_loop(0, n // 2 - 1, two, 0)
    gather(0, wb0, wb1, stage_b)
    finish(n - 1, stage_a)
    rrecv[0, 0:1], rrecv[0, 1:2] = reduce(stage_b)

    tracers = owner_ref.shape[1]
    rel = owner_ref[...] - me
    rel = jnp.where(rel < 0, rel + n, rel)
    onehot = jnp.where(iota((n, tracers), 0) == rel, 1.0, 0.0)
    placed = (iota((LANES, tracers), 0) % HALF) == rank_ref[...]
    placed = jnp.where(placed, 1.0, 0.0).astype(jnp.bfloat16)
    steps = counts_ref[...]
    h = 1.0 / jnp.maximum(steps, 1).astype(jnp.float32)
    dist = dist_ref[...]
    bins = dist.shape[0]
    both = wide(jnp.concatenate([kernel_ref[...], shatter_ref[...]], axis=0))
    moved = wide(redist_ref[...])

    def products(dist):
        out = mxu(both, tall(dist))
        dot, broken = out[:bins], out[bins:]
        return dot, broken, mxu(moved, tall(dist * dot))

    ready = products(dist)
    for d in range(1, n):
        back(d).wait()

    pair, single = rrecv[:, 0, :], rrecv[:, 1, :]
    spread = jnp.concatenate(
        [
            jnp.where(in_low, pair, 0.0),
            jnp.where(in_low, 0.0, pair),
            jnp.where(in_low, single, 0.0),
        ],
        axis=0,
    )
    found = sum(mxu(p, placed) for p in pieces(spread))
    sampled = [
        jnp.sum(found[f * n : (f + 1) * n] * onehot, axis=0, keepdims=True) for f in range(3)
    ]
    coag = sampled[0] * jnp.sqrt(sampled[1])
    shat = sampled[2] * sampled[1]
    for section in range(STEPS):
        dot, broken, spilt = ready if section == 0 else products(dist)
        gain = coag * spilt + shat * broken
        loss = coag * dot + shat
        fresh = (dist + h * gain) / (1.0 + h * loss)
        dist = jnp.where(steps >= section + 1, fresh, dist)
    out_ref[...] = dist


def shards(grid, distribution, owner_ids, coords, fracs, counts, kernel, redist, shatter):
    n = lax.axis_size("brick")
    bins, tracers = distribution.shape
    cap = 2 * tracers // n
    assert cap <= HALF and n % 2 == 0 and tracers % LANES == 0
    vmem = pl.BlockSpec(memory_space=pltpu.VMEM)
    f32 = jnp.float32
    hbm = pl.BlockSpec(memory_space=pltpu.HBM)
    kept = (
        jnp.swapaxes(grid.reshape(grid.shape[0], -1, LANES), 0, 1),
        counts.reshape(1, tracers), distribution, kernel, redist, shatter,
    )
    assert len(kept) == KEPT
    got, index, rank, owner, *kept = pl.pallas_call(
        functools.partial(request, n),
        out_shape=(
            jax.ShapeDtypeStruct((n, 4, LANES), f32),
            jax.ShapeDtypeStruct((2 * n, LANES), jnp.int32),
            jax.ShapeDtypeStruct((1, tracers), jnp.int32),
            jax.ShapeDtypeStruct((1, tracers), jnp.int32),
            *[jax.ShapeDtypeStruct(x.shape, x.dtype) for x in kept],
        ),
        in_specs=[hbm] * (3 + KEPT),
        out_specs=(vmem,) * (4 + KEPT),
        scratch_shapes=[
            pltpu.VMEM(coords.shape, jnp.int32),
            pltpu.VMEM(fracs.shape, f32),
            pltpu.VMEM((2, 8, tracers), f32),
            pltpu.VMEM((n, 4, LANES), f32),
            pltpu.VMEM((n, 4, LANES), f32),
            pltpu.SemaphoreType.DMA((3 + KEPT,)),
            pltpu.SemaphoreType.DMA((n,)),
            pltpu.SemaphoreType.DMA((n,)),
        ],
        compiler_params=pltpu.CompilerParams(
            collective_id=0, has_side_effects=True, vmem_limit_bytes=16 * 1024 * 1024
        ),
        name="request",
    )(*[pltpu.with_memory_space_constraint(x, pltpu.HBM) for x in (owner_ids.reshape(1, tracers), coords, fracs, *kept)])
    return pl.pallas_call(
        functools.partial(answer, n, cap),
        out_shape=jax.ShapeDtypeStruct((bins, tracers), f32),
        in_specs=[vmem] * (4 + KEPT),
        out_specs=vmem,
        scratch_shapes=[
            pltpu.SMEM((2 * n, LANES), jnp.int32),
            *[pltpu.VMEM((cap, LANES), f32)] * 4,
            *[pltpu.VMEM((3 * HALF, LANES), f32)] * 2,
            pltpu.VMEM((n, 2, LANES), f32),
            pltpu.VMEM((n, 2, LANES), f32),
            pltpu.SemaphoreType.DMA,
            pltpu.SemaphoreType.DMA((n,)),
            pltpu.SemaphoreType.DMA((n,)),
        ],
        compiler_params=pltpu.CompilerParams(
            collective_id=1, has_side_effects=True, vmem_limit_bytes=24 * 1024 * 1024
        ),
        name="answer",
    )(index, got, rank, owner, *kept)


def solution(mesh):
    in_specs = (
        P(None, ("runs", "brick")),
        P(None, ("runs", "brick")),
        P(("runs", "brick"), None),
        P(None, ("runs", "brick")),
        P(None, ("runs", "brick")),
        P(("runs", "brick")),
        P(),
        P(),
        P(),
    )
    out_specs = P(None, ("runs", "brick"))
    return jax.shard_map(shards, mesh=mesh, in_specs=in_specs, out_specs=out_specs, check_vma=False)
```

```python
import functools

import jax
import jax.numpy as jnp
from jax import lax
from jax.experimental import pallas as pl
from jax.experimental.pallas import tpu as pltpu
from jax.sharding import PartitionSpec as P

BS = 64
LANES = 128
HALF = LANES // 2
STEPS = 4
KEPT = 6
CHUNK = 32
MESH = pl.DeviceIdType.MESH


def iota(shape, dim):
    return lax.broadcasted_iota(jnp.int32, shape, dim)


def pieces(x, count=3):
    out = []
    for _ in range(count):
        high = x.astype(jnp.bfloat16)
        out.append(high)
        x = x - high.astype(jnp.float32)
    return out


def mxu(a, b, contract=((1,), (0,))):
    return lax.dot_general(a, b, (contract, ((), ())), preferred_element_type=jnp.float32)


NT = ((1,), (1,))


def wide(x):
    high, low = pieces(x, 2)
    return jnp.concatenate([high, high, low], axis=1)


def tall(x):
    high, low = pieces(x, 2)
    return jnp.concatenate([high, low, high], axis=0)


def partner(me, d, n):
    return {"brick": lax.rem(me + d, n)}


def greet(me, n):
    barrier = pltpu.get_barrier_semaphore()
    for d in range(1, n):
        pl.semaphore_signal(barrier, inc=1, device_id=partner(me, d, n), device_id_type=MESH)
    return barrier


def request(
    n, cap, owner_hbm, coords_hbm, fracs_hbm, *refs,
):
    kept_hbm = refs[:KEPT]
    w0_ref, w1_ref, index_ref, rank_ref, owner_ref = refs[KEPT : KEPT + 5]
    kept_refs = refs[KEPT + 5 : 2 * KEPT + 5]
    coords_ref, fracs_ref, pad, send, recv, load_sem, send_sem, recv_sem = refs[2 * KEPT + 5 :]
    me = lax.axis_index("brick")
    sources = (owner_hbm, coords_hbm, fracs_hbm) + kept_hbm
    table = kept_refs[0]
    cell_rows = kept_hbm[0].shape[0]
    targets = (owner_ref, coords_ref, fracs_ref, table.at[:cell_rows]) + kept_refs[1:]
    loads = [
        pltpu.make_async_copy(a, b, load_sem.at[i]) for i, (a, b) in enumerate(zip(sources, targets))
    ]
    for load in loads:
        load.start()
    barrier = greet(me, n)
    for load in loads[:3]:
        load.wait()

    tracers = owner_ref.shape[1]
    rel = owner_ref[...] - me
    rel = jnp.where(rel < 0, rel + n, rel)
    onehot = jnp.where(iota((n, tracers), 0) == rel, 1.0, 0.0)
    upto = jnp.where(iota((LANES, LANES), 0) <= iota((LANES, LANES), 1), 1.0, 0.0)
    upto = upto.astype(jnp.bfloat16)
    running = jnp.zeros((n, 1), jnp.float32)
    ranks = []
    for start in range(0, tracers, LANES):
        part = onehot[:, start : start + LANES]
        counted = mxu(part.astype(jnp.bfloat16), upto) + running
        running = counted[:, LANES - 1 :]
        ranks.append(jnp.sum(part * counted, axis=0, keepdims=True))
    rank = jnp.concatenate(ranks, axis=1).astype(jnp.int32) - 1
    rank_ref[...] = rank
    placed = (iota((LANES, tracers), 0) % HALF) == rank
    placed = jnp.where(placed, 1.0, 0.0).astype(jnp.bfloat16)

    pad[...] = jnp.zeros_like(pad)
    for row in (0, 4):
        pad[0, row : row + 3, :] = coords_ref[...].astype(jnp.float32)
        pad[1, row : row + 3, :] = fracs_ref[...]
    dest = (iota((4 * n, tracers), 0) // 4) == rel
    rows = [pad[0].astype(jnp.bfloat16)] + pieces(pad[1])
    left = []
    for x in rows:
        x = jnp.concatenate([x.astype(jnp.float32)] * (n // 2), axis=0)
        left.append(jnp.where(dest, x, 0.0).astype(jnp.bfloat16))
    packed = mxu(jnp.concatenate(left, axis=0), placed, NT)
    four = 4 * n
    packed = jnp.where(
        iota((four, LANES), 1) < HALF,
        packed[:four],
        packed[four : 2 * four] + packed[2 * four : 3 * four] + packed[3 * four :],
    )
    for d in range(n):
        send[d] = packed[4 * d : 4 * d + 4]
    recv[0] = packed[:4]

    pl.semaphore_wait(barrier, n - 1)
    copies = []
    for d in range(1, n):
        copy = pltpu.make_async_remote_copy(
            src_ref=send.at[d],
            dst_ref=recv.at[d],
            send_sem=send_sem.at[d],
            recv_sem=recv_sem.at[d],
            device_id=partner(me, d, n),
            device_id_type=MESH,
        )
        copy.start()
        copies.append(copy)

    loads[3].wait()
    front = iota((CHUNK,) + table.shape[1:], 2) < HALF

    def merge(i, carry):
        at = i * CHUNK
        here, after = table[pl.ds(at, CHUNK)], table[pl.ds(at + 1, CHUNK)]
        table[pl.ds(cell_rows + at, CHUNK)] = jnp.where(front, after, here)
        return carry

    lax.fori_loop(0, cell_rows // CHUNK, merge, 0)

    lanes = iota((cap, LANES), 1)
    inner = (lanes % HALF).astype(jnp.float32)
    lower = lanes < HALF

    def weigh(d):
        block = recv[d]
        turned = pltpu.roll(block, HALF, 1)
        odd = (block.astype(jnp.int32) & 1) == 1
        even = jnp.where(odd, turned, 1.0 - turned)
        columns = jnp.concatenate([block, even], axis=0).T
        ck = columns[:cap, 2:3]
        ae = columns[:cap, 5:6]
        a0 = columns[HALF : HALF + cap, 0:1]
        a2 = columns[HALF : HALF + cap, 2:3]
        w = jnp.where(inner == ck, 1.0 - a2, jnp.where(inner == ck + 1.0, a2, 0.0))
        w = w * jnp.where(lower, ae, 1.0 - ae)
        w0_ref[d * cap : (d + 1) * cap, :] = w * (1.0 - a0)
        w1_ref[d * cap : (d + 1) * cap, :] = w * a0

    order = [0]
    for near in range(1, n // 2 + 1):
        order += sorted({near, n - near})
    for start in range(0, n, 4):
        for d in order[start : start + 4]:
            if d:
                copies[d - 1].wait()
        for d in order[start : start + 4]:
            weigh(d)
    low = iota((n, LANES), 1) < HALF
    ci = jnp.where(low, recv[:, 0, :], 0.0).astype(jnp.int32)
    cj = jnp.where(low, recv[:, 1, :], 0.0).astype(jnp.int32)
    index_ref[...] = ci * (BS * BS // LANES) + (cj >> 1) + (cj & 1) * cell_rows
    for load in loads[4:]:
        load.wait()


def answer(
    n, cap, w0_ref, w1_ref, index_ref, rank_ref, owner_ref, table, counts_ref, dist_ref, kernel_ref,
    redist_ref, shatter_ref, out_ref,
    index_s, stage_a, stage_b, rsend, rrecv, index_sem, rsend_sem, rrecv_sem,
):
    me = lax.axis_index("brick")
    index_copy = pltpu.make_async_copy(index_ref, index_s, index_sem)
    index_copy.start()
    barrier = greet(me, n)
    in_low = iota((n, LANES), 1) < HALF
    plane = BS * BS // LANES
    ones = jnp.ones((8, 2 * LANES), jnp.bfloat16)

    def gather(d, stage):
        for c in range(cap):
            at = index_s[d, c]
            row = d * cap + c
            stage[c] = (
                table[at] * w0_ref[pl.ds(row, 1), :] + table[at + plane] * w1_ref[pl.ds(row, 1), :]
            )

    def reduce(stage):
        rows = []
        for f in range(3):
            rows.append(stage[:, f, :])
            if cap < HALF:
                rows.append(jnp.zeros((HALF - cap, LANES), jnp.float32))
        rows.append(jnp.zeros((HALF, LANES), jnp.float32))
        rows = jnp.concatenate(rows, axis=0)
        total = mxu(ones, jnp.concatenate(pieces(rows, 2), axis=1), NT)[:1]
        return total[:, :LANES], total[:, LANES:]

    def back(d):
        return pltpu.make_async_remote_copy(
            src_ref=rsend.at[d],
            dst_ref=rrecv.at[d],
            send_sem=rsend_sem.at[d],
            recv_sem=rrecv_sem.at[d],
            device_id=partner(me, n - d, n),
            device_id_type=MESH,
        )

    def finish(d, stage):
        rsend[d, 0:1], rsend[d, 1:2] = reduce(stage)
        back(d).start()

    index_copy.wait()
    gather(1, stage_a)
    pl.semaphore_wait(barrier, n - 1)

    def two(i, carry):
        d = 2 * i + 2
        gather(d, stage_b)
        finish(d - 1, stage_a)
        gather(d + 1, stage_a)
        finish(d, stage_b)
        return carry

    lax.fori_loop(0, n // 2 - 1, two, 0)
    gather(0, stage_b)
    finish(n - 1, stage_a)
    rrecv[0, 0:1], rrecv[0, 1:2] = reduce(stage_b)

    tracers = owner_ref.shape[1]
    rel = owner_ref[...] - me
    rel = jnp.where(rel < 0, rel + n, rel)
    onehot = jnp.where(iota((n, tracers), 0) == rel, 1.0, 0.0)
    placed = (iota((LANES, tracers), 0) % HALF) == rank_ref[...]
    placed = jnp.where(placed, 1.0, 0.0).astype(jnp.bfloat16)
    steps = counts_ref[...]
    h = 1.0 / jnp.maximum(steps, 1).astype(jnp.float32)
    dist = dist_ref[...]
    bins = dist.shape[0]
    both = wide(jnp.concatenate([kernel_ref[...], shatter_ref[...]], axis=0))
    moved = wide(redist_ref[...])

    def products(dist):
        out = mxu(both, tall(dist))
        dot, broken = out[:bins], out[bins:]
        return dot, broken, mxu(moved, tall(dist * dot))

    ready = products(dist)
    for d in range(1, n):
        back(d).wait()

    pair, single = rrecv[:, 0, :], rrecv[:, 1, :]
    spread = jnp.concatenate(
        [
            jnp.where(in_low, pair, 0.0),
            jnp.where(in_low, 0.0, pair),
            jnp.where(in_low, single, 0.0),
        ],
        axis=0,
    )
    found = sum(mxu(p, placed) for p in pieces(spread))
    sampled = [
        jnp.sum(found[f * n : (f + 1) * n] * onehot, axis=0, keepdims=True) for f in range(3)
    ]
    coag = sampled[0] * jnp.sqrt(sampled[1])
    shat = sampled[2] * sampled[1]
    for section in range(STEPS):
        dot, broken, spilt = ready if section == 0 else products(dist)
        gain = coag * spilt + shat * broken
        loss = coag * dot + shat
        fresh = (dist + h * gain) / (1.0 + h * loss)
        dist = jnp.where(steps >= section + 1, fresh, dist)
    out_ref[...] = dist


def shards(grid, distribution, owner_ids, coords, fracs, counts, kernel, redist, shatter):
    n = lax.axis_size("brick")
    bins, tracers = distribution.shape
    cap = 2 * tracers // n
    assert cap <= HALF and n % 2 == 0 and tracers % LANES == 0
    vmem = pl.BlockSpec(memory_space=pltpu.VMEM)
    f32 = jnp.float32
    hbm = pl.BlockSpec(memory_space=pltpu.HBM)
    kept = (
        jnp.swapaxes(grid.reshape(grid.shape[0], -1, LANES), 0, 1),
        counts.reshape(1, tracers), distribution, kernel, redist, shatter,
    )
    assert len(kept) == KEPT
    table = jax.ShapeDtypeStruct((2 * kept[0].shape[0], *kept[0].shape[1:]), f32)
    w0, w1, index, rank, owner, *kept = pl.pallas_call(
        functools.partial(request, n, cap),
        out_shape=(
            jax.ShapeDtypeStruct((n * cap, LANES), f32),
            jax.ShapeDtypeStruct((n * cap, LANES), f32),
            jax.ShapeDtypeStruct((n, LANES), jnp.int32),
            jax.ShapeDtypeStruct((1, tracers), jnp.int32),
            jax.ShapeDtypeStruct((1, tracers), jnp.int32),
            table,
            *[jax.ShapeDtypeStruct(x.shape, x.dtype) for x in kept[1:]],
        ),
        in_specs=[hbm] * (3 + KEPT),
        out_specs=(vmem,) * (5 + KEPT),
        scratch_shapes=[
            pltpu.VMEM(coords.shape, jnp.int32),
            pltpu.VMEM(fracs.shape, f32),
            pltpu.VMEM((2, 8, tracers), f32),
            pltpu.VMEM((n, 4, LANES), f32),
            pltpu.VMEM((n, 4, LANES), f32),
            pltpu.SemaphoreType.DMA((3 + KEPT,)),
            pltpu.SemaphoreType.DMA((n,)),
            pltpu.SemaphoreType.DMA((n,)),
        ],
        compiler_params=pltpu.CompilerParams(
            collective_id=0, has_side_effects=True, vmem_limit_bytes=16 * 1024 * 1024
        ),
        name="request",
    )(*[pltpu.with_memory_space_constraint(x, pltpu.HBM) for x in (owner_ids.reshape(1, tracers), coords, fracs, *kept)])
    return pl.pallas_call(
        functools.partial(answer, n, cap),
        out_shape=jax.ShapeDtypeStruct((bins, tracers), f32),
        in_specs=[vmem] * (5 + KEPT),
        out_specs=vmem,
        scratch_shapes=[
            pltpu.SMEM((n, LANES), jnp.int32),
            *[pltpu.VMEM((cap, 3, LANES), f32)] * 2,
            pltpu.VMEM((n, 2, LANES), f32),
            pltpu.VMEM((n, 2, LANES), f32),
            pltpu.SemaphoreType.DMA,
            pltpu.SemaphoreType.DMA((n,)),
            pltpu.SemaphoreType.DMA((n,)),
        ],
        compiler_params=pltpu.CompilerParams(
            collective_id=1, has_side_effects=True, vmem_limit_bytes=24 * 1024 * 1024
        ),
        name="answer",
    )(w0, w1, index, rank, owner, *kept)


def solution(mesh):
    in_specs = (
        P(None, ("runs", "brick")),
        P(None, ("runs", "brick")),
        P(("runs", "brick"), None),
        P(None, ("runs", "brick")),
        P(None, ("runs", "brick")),
        P(("runs", "brick")),
        P(),
        P(),
        P(),
    )
    out_specs = P(None, ("runs", "brick"))
    return jax.shard_map(shards, mesh=mesh, in_specs=in_specs, out_specs=out_specs, check_vma=False)
```

```python
import functools

import jax
import jax.numpy as jnp
from jax import lax
from jax.experimental import pallas as pl
from jax.experimental.pallas import tpu as pltpu
from jax.sharding import PartitionSpec as P

BS = 64
LANES = 128
HALF = LANES // 2
STEPS = 4
KEPT = 6
GROUPS = 4
MESH = pl.DeviceIdType.MESH


def iota(shape, dim):
    return lax.broadcasted_iota(jnp.int32, shape, dim)


def pieces(x, count=3):
    out = []
    for _ in range(count):
        high = x.astype(jnp.bfloat16)
        out.append(high)
        x = x - high.astype(jnp.float32)
    return out


def mxu(a, b, contract=((1,), (0,))):
    return lax.dot_general(a, b, (contract, ((), ())), preferred_element_type=jnp.float32)


NT = ((1,), (1,))


def wide(x):
    high, low = pieces(x, 2)
    return jnp.concatenate([high, high, low], axis=1)


def tall(x):
    high, low = pieces(x, 2)
    return jnp.concatenate([high, low, high], axis=0)


def partner(me, d, n):
    return {"brick": lax.rem(me + d, n)}


def greet(me, n):
    barrier = pltpu.get_barrier_semaphore()
    for d in range(1, n):
        pl.semaphore_signal(barrier, inc=1, device_id=partner(me, d, n), device_id_type=MESH)
    return barrier


def request(
    n, owner_hbm, coords_hbm, fracs_hbm, *refs,
):
    kept_hbm, (got_ref, index_ref, rank_ref, owner_ref) = refs[:KEPT], refs[KEPT : KEPT + 4]
    kept_refs = refs[KEPT + 4 : 2 * KEPT + 4]
    coords_ref, fracs_ref, pad, send, recv, load_sem, send_sem, recv_sem = refs[2 * KEPT + 4 :]
    me = lax.axis_index("brick")
    sources = (owner_hbm, coords_hbm, fracs_hbm) + kept_hbm
    targets = (owner_ref, coords_ref, fracs_ref) + kept_refs
    loads = [
        pltpu.make_async_copy(a, b, load_sem.at[i]) for i, (a, b) in enumerate(zip(sources, targets))
    ]
    for load in loads:
        load.start()
    barrier = greet(me, n)
    for load in loads[:3]:
        load.wait()

    tracers = owner_ref.shape[1]
    rel = owner_ref[...] - me
    rel = jnp.where(rel < 0, rel + n, rel)
    onehot = jnp.where(iota((n, tracers), 0) == rel, 1.0, 0.0)
    upto = jnp.where(iota((LANES, LANES), 0) <= iota((LANES, LANES), 1), 1.0, 0.0)
    upto = upto.astype(jnp.bfloat16)
    running = jnp.zeros((n, 1), jnp.float32)
    ranks = []
    for start in range(0, tracers, LANES):
        part = onehot[:, start : start + LANES]
        counted = mxu(part.astype(jnp.bfloat16), upto) + running
        running = counted[:, LANES - 1 :]
        ranks.append(jnp.sum(part * counted, axis=0, keepdims=True))
    rank = jnp.concatenate(ranks, axis=1).astype(jnp.int32) - 1
    rank_ref[...] = rank
    placed = (iota((LANES, tracers), 0) % HALF) == rank
    placed = jnp.where(placed, 1.0, 0.0).astype(jnp.bfloat16)

    pad[...] = jnp.zeros_like(pad)
    for row in (0, 4):
        pad[0, row : row + 3, :] = coords_ref[...].astype(jnp.float32)
        pad[1, row : row + 3, :] = fracs_ref[...]
    dest = (iota((4 * n, tracers), 0) // 4) == rel
    rows = [pad[0].astype(jnp.bfloat16)] + pieces(pad[1])
    left = []
    for x in rows:
        x = jnp.concatenate([x.astype(jnp.float32)] * (n // 2), axis=0)
        left.append(jnp.where(dest, x, 0.0).astype(jnp.bfloat16))
    packed = mxu(jnp.concatenate(left, axis=0), placed, NT)
    four = 4 * n
    packed = jnp.where(
        iota((four, LANES), 1) < HALF,
        packed[:four],
        packed[four : 2 * four] + packed[2 * four : 3 * four] + packed[3 * four :],
    )
    for d in range(n):
        send[d] = packed[4 * d : 4 * d + 4]
    recv[0] = packed[:4]

    pl.semaphore_wait(barrier, n - 1)
    copies = []
    for d in range(1, n):
        copy = pltpu.make_async_remote_copy(
            src_ref=send.at[d],
            dst_ref=recv.at[d],
            send_sem=send_sem.at[d],
            recv_sem=recv_sem.at[d],
            device_id=partner(me, d, n),
            device_id_type=MESH,
        )
        copy.start()
        copies.append(copy)
    for copy in copies:
        copy.wait()

    low = iota((n, LANES), 1) < HALF
    ci = jnp.where(low, recv[:, 0, :], 0.0).astype(jnp.int32)
    cj = jnp.where(low, recv[:, 1, :], 0.0).astype(jnp.int32)
    base = ci * (BS * BS // LANES)
    index_ref[:n] = base + (cj >> 1)
    index_ref[n:] = base + ((cj + 1) >> 1)
    got_ref[...] = recv[...]
    for load in loads[3:]:
        load.wait()


def answer(
    n, cap, index_ref, got_ref, rank_ref, owner_ref, cells, counts_ref, dist_ref, kernel_ref,
    redist_ref, shatter_ref, out_ref,
    w0_ref, w1_ref, stage, rsend, rrecv, rsend_sem, rrecv_sem,
):
    me = lax.axis_index("brick")
    barrier = greet(me, n)

    first, second, third = got_ref[:, 0, :], got_ref[:, 1, :], got_ref[:, 2, :]
    in_low = iota((n, LANES), 1) < HALF
    cj = jnp.where(in_low, second, 0.0).astype(jnp.int32)
    f0 = pltpu.roll(first, HALF, 1)
    f1 = pltpu.roll(second, HALF, 1)
    f2 = pltpu.roll(third, HALF, 1)
    even = jnp.where((cj & 1) == 0, 1.0 - f1, f1)
    columns = jnp.concatenate([third, f2, even, f0], axis=0).T
    lanes = iota((cap, LANES), 1)
    inner = (lanes % HALF).astype(jnp.float32)
    lower = lanes < HALF
    for s in range(n):
        ck = columns[:cap, s : s + 1]
        a2 = columns[:cap, n + s : n + s + 1]
        ae = columns[:cap, 2 * n + s : 2 * n + s + 1]
        a0 = columns[:cap, 3 * n + s : 3 * n + s + 1]
        w = jnp.where(inner == ck, 1.0 - a2, jnp.where(inner == ck + 1.0, a2, 0.0))
        w = w * jnp.where(lower, ae, 1.0 - ae)
        w0_ref[s * cap : (s + 1) * cap, :] = w * (1.0 - a0)
        w1_ref[s * cap : (s + 1) * cap, :] = w * a0

    plane = BS * BS // LANES
    front = iota((3, LANES), 1) < HALF

    def one(s, carry):
        for c in range(cap):
            up = index_ref[s, c]
            dn = index_ref[n + s, c]
            near = jnp.where(front, cells[dn], cells[up])
            far = jnp.where(front, cells[dn + plane], cells[up + plane])
            at = s * cap + c
            acc = near * w0_ref[pl.ds(at, 1), :] + far * w1_ref[pl.ds(at, 1), :]
            stage[at] = acc
        return carry

    ones = jnp.ones((8, 2 * LANES), jnp.bfloat16)
    size = n // GROUPS
    copies = []
    for g in range(GROUPS):
        lax.fori_loop(g * size, (g + 1) * size, one, 0)
        for s in range(g * size, (g + 1) * size):
            rows = []
            for f in range(3):
                rows.append(stage[s * cap : (s + 1) * cap, f, :])
                if cap < HALF:
                    rows.append(jnp.zeros((HALF - cap, LANES), jnp.float32))
            rows.append(jnp.zeros((HALF, LANES), jnp.float32))
            rows = jnp.concatenate(pieces(jnp.concatenate(rows, axis=0), 2), axis=1)
            total = mxu(ones, rows, NT)[:1]
            rsend[s, 0:1] = total[:, :LANES]
            rsend[s, 1:2] = total[:, LANES:]
        if g == 0:
            pl.semaphore_wait(barrier, n - 1)
            rrecv[0] = rsend[0]
        for d in range(max(1, g * size), (g + 1) * size):
            copy = pltpu.make_async_remote_copy(
                src_ref=rsend.at[d],
                dst_ref=rrecv.at[d],
                send_sem=rsend_sem.at[d],
                recv_sem=rrecv_sem.at[d],
                device_id=partner(me, n - d, n),
                device_id_type=MESH,
            )
            copy.start()
            copies.append(copy)

    tracers = owner_ref.shape[1]
    rel = owner_ref[...] - me
    rel = jnp.where(rel < 0, rel + n, rel)
    onehot = jnp.where(iota((n, tracers), 0) == rel, 1.0, 0.0)
    placed = (iota((LANES, tracers), 0) % HALF) == rank_ref[...]
    placed = jnp.where(placed, 1.0, 0.0).astype(jnp.bfloat16)
    steps = counts_ref[...]
    h = 1.0 / jnp.maximum(steps, 1).astype(jnp.float32)
    dist = dist_ref[...]
    bins = dist.shape[0]
    both = wide(jnp.concatenate([kernel_ref[...], shatter_ref[...]], axis=0))
    moved = wide(redist_ref[...])

    def products(dist):
        out = mxu(both, tall(dist))
        dot, broken = out[:bins], out[bins:]
        return dot, broken, mxu(moved, tall(dist * dot))

    ready = products(dist)
    for copy in copies:
        copy.wait()

    pair, single = rrecv[:, 0, :], rrecv[:, 1, :]
    spread = jnp.concatenate(
        [
            jnp.where(in_low, pair, 0.0),
            jnp.where(in_low, 0.0, pair),
            jnp.where(in_low, single, 0.0),
        ],
        axis=0,
    )
    found = sum(mxu(p, placed) for p in pieces(spread))
    sampled = [
        jnp.sum(found[f * n : (f + 1) * n] * onehot, axis=0, keepdims=True) for f in range(3)
    ]
    coag = sampled[0] * jnp.sqrt(sampled[1])
    shat = sampled[2] * sampled[1]
    for section in range(STEPS):
        dot, broken, back = ready if section == 0 else products(dist)
        gain = coag * back + shat * broken
        loss = coag * dot + shat
        fresh = (dist + h * gain) / (1.0 + h * loss)
        dist = jnp.where(steps >= section + 1, fresh, dist)
    out_ref[...] = dist


def shards(grid, distribution, owner_ids, coords, fracs, counts, kernel, redist, shatter):
    n = lax.axis_size("brick")
    bins, tracers = distribution.shape
    cap = 2 * tracers // n
    assert cap <= HALF and n % 2 == 0 and tracers % LANES == 0
    vmem = pl.BlockSpec(memory_space=pltpu.VMEM)
    smem = pl.BlockSpec(memory_space=pltpu.SMEM)
    f32 = jnp.float32
    hbm = pl.BlockSpec(memory_space=pltpu.HBM)
    kept = (
        jnp.swapaxes(grid.reshape(grid.shape[0], -1, LANES), 0, 1),
        counts.reshape(1, tracers), distribution, kernel, redist, shatter,
    )
    assert len(kept) == KEPT
    got, index, rank, owner, *kept = pl.pallas_call(
        functools.partial(request, n),
        out_shape=(
            jax.ShapeDtypeStruct((n, 4, LANES), f32),
            jax.ShapeDtypeStruct((2 * n, LANES), jnp.int32),
            jax.ShapeDtypeStruct((1, tracers), jnp.int32),
            jax.ShapeDtypeStruct((1, tracers), jnp.int32),
            *[jax.ShapeDtypeStruct(x.shape, x.dtype) for x in kept],
        ),
        in_specs=[hbm] * (3 + KEPT),
        out_specs=(vmem,) * (4 + KEPT),
        scratch_shapes=[
            pltpu.VMEM(coords.shape, jnp.int32),
            pltpu.VMEM(fracs.shape, f32),
            pltpu.VMEM((2, 8, tracers), f32),
            pltpu.VMEM((n, 4, LANES), f32),
            pltpu.VMEM((n, 4, LANES), f32),
            pltpu.SemaphoreType.DMA((3 + KEPT,)),
            pltpu.SemaphoreType.DMA((n,)),
            pltpu.SemaphoreType.DMA((n,)),
        ],
        compiler_params=pltpu.CompilerParams(
            collective_id=0, has_side_effects=True, vmem_limit_bytes=16 * 1024 * 1024
        ),
        name="request",
    )(*[pltpu.with_memory_space_constraint(x, pltpu.HBM) for x in (owner_ids.reshape(1, tracers), coords, fracs, *kept)])
    return pl.pallas_call(
        functools.partial(answer, n, cap),
        out_shape=jax.ShapeDtypeStruct((bins, tracers), f32),
        in_specs=[smem] + [vmem] * (3 + KEPT),
        out_specs=vmem,
        scratch_shapes=[
            pltpu.VMEM((n * cap, LANES), f32),
            pltpu.VMEM((n * cap, LANES), f32),
            pltpu.VMEM((n * cap, 3, LANES), f32),
            pltpu.VMEM((n, 2, LANES), f32),
            pltpu.VMEM((n, 2, LANES), f32),
            pltpu.SemaphoreType.DMA((n,)),
            pltpu.SemaphoreType.DMA((n,)),
        ],
        compiler_params=pltpu.CompilerParams(
            collective_id=1, has_side_effects=True, vmem_limit_bytes=24 * 1024 * 1024
        ),
        name="answer",
    )(index, got, rank, owner, *kept)


def solution(mesh):
    in_specs = (
        P(None, ("runs", "brick")),
        P(None, ("runs", "brick")),
        P(("runs", "brick"), None),
        P(None, ("runs", "brick")),
        P(None, ("runs", "brick")),
        P(("runs", "brick")),
        P(),
        P(),
        P(),
    )
    out_specs = P(None, ("runs", "brick"))
    return jax.shard_map(shards, mesh=mesh, in_specs=in_specs, out_specs=out_specs, check_vma=False)
```
